256 devices in a mesh: chan: 64 (over y, x_hi, z), blk: 4 (over x_lo, core).
Axes of the slice: x: 4 (x_hi: 2, x_lo: 2; x = x_hi * 2 + x_lo), y: 4, z: 8, core: 2. Of those that a mesh axis runs over, the one named last changes fastest.
Arguments:
- voltages: int32 [1024, 262144], P('chan', 'blk'), may hold values from -127 to 127, as said below
Outputs:
- vis_real: float32 [256, 1024, 1024], P(('chan', 'blk'))
- vis_imag: float32 [256, 1024, 1024], P(('chan', 'blk'))
The draws below stay inside these ranges and needn't reach their ends.
Inputs may be any that keep to these rules, and one draw needn't show every extreme that they name: `voltages`: integer voltage samples.
All inputs are finite; a program needn't handle non-finite values.
Results may differ from the reference program's by a relative error of at most 0.004.
Values may be sent and summed in bfloat16 or wider, within the bound.
A program may use at most 64 MiB of HBM per device.

```python
import math
import jax
import jax.numpy as jnp
from jax import lax

NI = 1024
NC = 256
TAPS = 4
FFT = 512
FRAMES = 512
SAMPLES = 262144


def draw_voltages(key, part):
    key_signal = jax.random.fold_in(key, 101)
    key_sign = jax.random.fold_in(key, 202)
    key_noise = jax.random.fold_in(key, 303)
    signal = jax.random.randint(key_signal, (1, SAMPLES), -40, 41, dtype=jnp.int32)
    polarity = 2 * jax.random.randint(key_sign, (NI, 1), 0, 2, dtype=jnp.int32) - 1
    noise = jax.random.randint(key_noise, (NI, SAMPLES), -87, 88, dtype=jnp.int32)
    return polarity * signal + noise


def setup_inputs(seed: int = 0) -> dict:
    key_list = jax.random.split(jax.random.key(seed), 2)
    voltages = draw_voltages(jax.random.fold_in(key_list[1], 71), 0)
    return dict(voltages=voltages)


def build_taps():
    length = TAPS * FFT
    points = jnp.arange(length, dtype=jnp.float32)
    centre = (length - 1) / 2.0
    window = 0.54 - 0.46 * jnp.cos(2.0 * jnp.pi * points / (length - 1))
    return (jnp.sinc((points - centre) / FFT) * window).reshape(TAPS, FFT)

def spectrum_scale(filter_taps):
    energy = jnp.mean(lax.optimization_barrier(jnp.sum(filter_taps * filter_taps, axis=0)))
    return 1.0 / (56.0 * jnp.sqrt(FFT * energy))

def reference(voltages):
    filter_taps = build_taps()
    scale_factor = spectrum_scale(filter_taps)
    group_size = math.gcd(NI, 16)

    def one_group(group):
        samples = group.astype(jnp.float32).reshape(group_size, FRAMES, FFT)
        padded = jnp.concatenate([jnp.zeros((group_size, TAPS - 1, FFT), jnp.float32), samples], axis=1)
        filtered = jnp.zeros((group_size, FRAMES, FFT), jnp.float32)
        for offset in range(TAPS):
            filtered = filtered + filter_taps[offset] * padded[:, offset:offset + FRAMES, :]
        spectrum = jnp.fft.rfft(filtered, axis=-1)[:, :, :NC]
        real_part = (jnp.real(spectrum) * scale_factor).astype(jnp.bfloat16)
        imag_part = (jnp.imag(spectrum) * scale_factor).astype(jnp.bfloat16)
        return (real_part, imag_part)
    real_all, imag_all = lax.map(one_group, voltages.reshape(NI // group_size, group_size, SAMPLES))
    real_all = jnp.transpose(real_all.reshape(NI, FRAMES, NC), (2, 0, 1))
    imag_all = jnp.transpose(imag_all.reshape(NI, FRAMES, NC), (2, 0, 1))

    def one_channel(planes):
        real_rows = planes[0].astype(jnp.float32)
        imag_rows = planes[1].astype(jnp.float32)
        highest = lax.Precision.HIGHEST
        out_real = jnp.dot(real_rows, real_rows.T, precision=highest) + jnp.dot(imag_rows, imag_rows.T, precision=highest)
        out_imag = jnp.dot(imag_rows, real_rows.T, precision=highest) - jnp.dot(real_rows, imag_rows.T, precision=highest)
        return (out_real / FRAMES, out_imag / FRAMES)
    vis_real, vis_imag = lax.map(one_channel, (real_all, imag_all))
    return (vis_real, vis_imag)
```

```python
import functools

import jax
import jax.numpy as jnp
import numpy as np
from jax import lax
from jax.experimental import pallas as pl
from jax.experimental.pallas import tpu as pltpu
from jax.sharding import PartitionSpec as P

NI = 1024
NC = 256
TAPS = 4
FFT = 512
HALF = FFT // 2
HISTORY = TAPS - 1
MESH = pl.DeviceIdType.MESH


def shifted(value, axis, steps):
    count = lax.axis_size(axis)
    leading, last = (max(0, -steps), min(count, count - steps))
    return lax.ppermute(value, axis, [(source, source + steps) for source in range(leading, last)])


def tables():
    length = TAPS * FFT
    points = np.arange(length, dtype=np.float64)
    window = 0.54 - 0.46 * np.cos(2.0 * np.pi * points / (length - 1))
    taps = (np.sinc((points - (length - 1) / 2.0) / FFT) * window).reshape(TAPS, FFT)
    scale = 1.0 / (56.0 * np.sqrt(FFT * np.mean(np.sum(taps * taps, axis=0))))
    weights = []
    for parity in range(2):
        channel = np.arange(parity, NC, 2)[:, None]
        angle = (channel * np.arange(HALF)[None, :] % FFT) * (2.0 * np.pi / FFT)
        matrix = (scale * np.concatenate([np.cos(angle), -np.sin(angle)], axis=0)).astype(np.float32)
        high = matrix.astype(jnp.bfloat16)
        low = (matrix - high.astype(np.float32)).astype(jnp.bfloat16)
        weights.append(np.concatenate([high, high, low], axis=1))
    return taps.astype(np.float32), np.stack(weights)


def exchange_kernel(frames, v_hbm, halo_hbm, taps_ref, w_ref, x_ref, vb, fold, turn, spec, in_sem, send_sem, recv_sem):
    inputs = v_hbm.shape[0]
    chan = lax.axis_index("chan")
    blk = lax.axis_index("blk")
    chunks = in_sem.shape[0] - 1
    per = frames // chunks
    lead = HISTORY * FFT
    loads = [pltpu.make_async_copy(halo_hbm, vb.at[:, pl.ds(0, lead)], in_sem.at[chunks])]
    for c in range(chunks):
        span = per * FFT
        loads.append(
            pltpu.make_async_copy(
                v_hbm.at[:, pl.ds(c * span, span)], vb.at[:, pl.ds(lead + c * span, span)], in_sem.at[c]
            )
        )
    for load in loads:
        load.start()

    z = chan & 7
    y = (chan >> 4) & 3
    x = ((chan >> 3) & 1) * 2 + (blk >> 1)
    core = blk & 1

    def place(dx, dy, dz, dc):
        tx = (x + dx) & 3
        tc = (((y + dy) & 3) << 4) | ((tx >> 1) << 3) | ((z + dz) & 7)
        tb = ((tx & 1) << 1) | (core ^ dc)
        return tc, tb

    barrier = pltpu.get_barrier_semaphore()

    def greet(r, _):
        for dz in range(8):
            tc, tb = place(r & 3, (r >> 2) & 3, dz, r >> 4)

            def signal():
                pl.semaphore_signal(barrier, inc=1, device_id=(tc, tb), device_id_type=MESH)

            if dz:
                signal()
            else:
                pl.when(r > 0)(signal)
        return 0

    lax.fori_loop(0, 32, greet, 0)

    taps = [taps_ref[pl.ds(t, 1), :] for t in range(TAPS)]

    def sample(f):
        return vb[:, pl.ds(pl.multiple_of(f * FFT, FFT), FFT)].astype(jnp.float32)

    def filter_frames(g, window):
        window = list(window)
        for u in range(4):
            f = g * 4 + u
            window.append(sample(f + HISTORY))
            value = taps[0] * window[0]
            for t in range(1, TAPS):
                value = value + taps[t] * window[t]
            window = window[1:]
            folded = (value[:, :HALF] + value[:, HALF:], value[:, :HALF] - value[:, HALF:])
            for parity in range(2):
                for lane in range(HALF // 128):
                    fold[parity * 2 + lane, pl.ds(f, inputs, stride=frames), :] = folded[parity][
                        :, lane * 128 : (lane + 1) * 128
                    ]
        return tuple(window)

    loads[0].wait()
    window = tuple(sample(f) for f in range(HISTORY))
    for c in range(chunks):
        loads[c + 1].wait()
        window = lax.fori_loop(c * per // 4, (c + 1) * per // 4, filter_frames, window)

    pair = 2 * frames

    def transform(p, _):
        rows = pl.ds(pl.multiple_of(p * pair, pair), pair)
        for parity in range(2):
            value = jnp.concatenate([fold[parity * 2, rows, :], fold[parity * 2 + 1, rows, :]], axis=1)
            high = value.astype(jnp.bfloat16)
            low = (value - high.astype(jnp.float32)).astype(jnp.bfloat16)
            out = lax.dot_general(
                w_ref[parity],
                jnp.concatenate([high, low, high], axis=1),
                (((1,), (1,)), ((), ())),
                preferred_element_type=jnp.float32,
            )
            for h in range(2):
                for part in range(2):
                    start = parity * 2 * inputs + part * inputs + p * 2 + h
                    turn[pl.ds(start, NC // 2, stride=4 * inputs), :] = out[
                        part * NC // 2 : (part + 1) * NC // 2, h * frames : (h + 1) * frames
                    ]
        return 0

    lax.fori_loop(0, inputs // 2, transform, 0)

    def pack(g, _):
        for u in range(8):
            k = g * 8 + u
            both = turn[pl.ds(pl.multiple_of(k * 2 * inputs, 2 * inputs), 2 * inputs), :].astype(jnp.bfloat16)
            spec[k, :, 0:frames] = both[0:inputs]
            spec[k, :, frames : 2 * frames] = both[inputs : 2 * inputs]
        return 0

    lax.fori_loop(0, NC // 8, pack, 0)

    pl.semaphore_wait(barrier, 255)
    row = pl.ds(pl.multiple_of(chan * inputs, inputs), inputs)
    col = pl.ds(pl.multiple_of(blk * pair, pair), pair)
    pltpu.make_async_copy(spec.at[chan * 4 + blk], x_ref.at[row, col], recv_sem).start()

    def send(r, _):
        for dz in range(8):
            tc, tb = place(r & 3, (r >> 2) & 3, dz, r >> 4)

            def copy():
                pltpu.make_async_remote_copy(
                    src_ref=spec.at[tc * 4 + tb],
                    dst_ref=x_ref.at[row, col],
                    send_sem=send_sem,
                    recv_sem=recv_sem,
                    device_id=(tc, tb),
                    device_id_type=MESH,
                ).start()

            if dz:
                copy()
            else:
                pl.when(r > 0)(copy)
        return 0

    lax.fori_loop(0, 32, send, 0)
    pltpu.make_async_copy(spec.at[pl.ds(0, NC - 1)], spec.at[pl.ds(0, NC - 1)], send_sem).wait()
    pltpu.make_async_copy(x_ref, x_ref, recv_sem).wait()


def exchange(voltages, halo, taps, weights):
    inputs, samples = voltages.shape
    frames = samples // FFT
    chunks = 4
    hbm = pl.BlockSpec(memory_space=pl.ANY)
    vmem = pl.BlockSpec(memory_space=pltpu.VMEM)
    return pl.pallas_call(
        functools.partial(exchange_kernel, frames),
        out_shape=jax.ShapeDtypeStruct((NI, 8 * frames), jnp.bfloat16),
        in_specs=[hbm, hbm, vmem, vmem],
        out_specs=hbm,
        scratch_shapes=[
            pltpu.VMEM((inputs, HISTORY * FFT + samples), jnp.int32),
            pltpu.VMEM((FFT // 128, inputs * frames, 128), jnp.float32),
            pltpu.VMEM((NC * 2 * inputs, frames), jnp.float32),
            pltpu.VMEM((NC, inputs, 2 * frames), jnp.bfloat16),
            pltpu.SemaphoreType.DMA((chunks + 1,)),
            pltpu.SemaphoreType.DMA,
            pltpu.SemaphoreType.DMA,
        ],
        compiler_params=pltpu.CompilerParams(
            collective_id=0, has_side_effects=True, vmem_limit_bytes=40 * 1024 * 1024
        ),
        name="filterbank_exchange",
    )(voltages, halo, taps, weights)


def correlate_kernel(frames, total, a_ref, x_ref, re_ref, im_ref):
    left = a_ref[...]
    pieces = []
    for block in range(left.shape[1] // (2 * frames)):
        start = block * 2 * frames
        pieces.append(left[:, start + frames : start + 2 * frames])
        pieces.append(-left[:, start : start + frames])
    swapped = jnp.concatenate(pieces, axis=1)
    contract = (((1,), (1,)), ((), ()))
    right = x_ref[...]
    scale = 1.0 / total
    re_ref[0] = lax.dot_general(left, right, contract, preferred_element_type=jnp.float32) * scale
    im_ref[0] = lax.dot_general(swapped, right, contract, preferred_element_type=jnp.float32) * scale


def correlate(turned, frames):
    rows, depth = turned.shape
    step = 128
    shape = jax.ShapeDtypeStruct((1, rows, rows), jnp.float32)
    out = pl.BlockSpec((1, step, rows), lambda i: (0, i, 0))
    return pl.pallas_call(
        functools.partial(correlate_kernel, frames, depth // 2),
        out_shape=(shape, shape),
        grid=(rows // step,),
        in_specs=[
            pl.BlockSpec((step, depth), lambda i: (i, 0)),
            pl.BlockSpec((rows, depth), lambda i: (0, 0), pipeline_mode=pl.Buffered(1)),
        ],
        out_specs=(out, out),
        compiler_params=pltpu.CompilerParams(vmem_limit_bytes=40 * 1024 * 1024),
        name="correlate",
    )(turned, turned)


def local(voltages):
    frames = voltages.shape[1] // FFT
    taps, weights = tables()
    tail = voltages[:, (frames - HISTORY) * FFT :]
    halo = shifted(tail, "blk", 1)
    turned = exchange(voltages, halo, jnp.asarray(taps), jnp.asarray(weights))
    return correlate(turned, frames)


def solution(mesh):
    return jax.shard_map(
        local,
        mesh=mesh,
        in_specs=(P("chan", "blk"),),
        out_specs=(P(("chan", "blk"), None, None), P(("chan", "blk"), None, None)),
        check_vma=False,
    )
```

```python
import functools

import jax
import jax.numpy as jnp
import numpy as np
from jax import lax
from jax.experimental import pallas as pl
from jax.experimental.pallas import tpu as pltpu
from jax.sharding import PartitionSpec as P

NI = 1024
NC = 256
TAPS = 4
FFT = 512
HALF = FFT // 2
HISTORY = TAPS - 1
MESH = pl.DeviceIdType.MESH


def shifted(value, axis, steps):
    count = lax.axis_size(axis)
    leading, last = (max(0, -steps), min(count, count - steps))
    return lax.ppermute(value, axis, [(source, source + steps) for source in range(leading, last)])


def tables():
    length = TAPS * FFT
    points = np.arange(length, dtype=np.float64)
    window = 0.54 - 0.46 * np.cos(2.0 * np.pi * points / (length - 1))
    taps = (np.sinc((points - (length - 1) / 2.0) / FFT) * window).reshape(TAPS, FFT)
    scale = 1.0 / (56.0 * np.sqrt(FFT * np.mean(np.sum(taps * taps, axis=0))))
    weights = []
    for parity in range(2):
        channel = np.arange(parity, NC, 2)[:, None]
        angle = (channel * np.arange(HALF)[None, :] % FFT) * (2.0 * np.pi / FFT)
        matrix = (scale * np.concatenate([np.cos(angle), -np.sin(angle)], axis=0)).astype(np.float32)
        high = matrix.astype(jnp.bfloat16)
        low = (matrix - high.astype(np.float32)).astype(jnp.bfloat16)
        weights.append(np.concatenate([high, high, low], axis=1))
    return taps.astype(np.float32), np.stack(weights)


FOLD_PITCH = 132
TURN_PITCH = 36


def exchange_kernel(
    frames,
    v_hbm,
    halo_hbm,
    taps_hbm,
    w_hbm,
    last_ref,
    re_ref,
    im_ref,
    vb,
    taps_ref,
    w_ref,
    fold,
    turn,
    spec,
    landed,
    in_sem,
    send_sem,
    recv_sem,
):
    inputs = v_hbm.shape[0]
    chan = lax.axis_index("chan")
    blk = lax.axis_index("blk")
    chunks = in_sem.shape[0] - 3
    per = frames // chunks
    lead = HISTORY * FFT
    table_loads = [
        pltpu.make_async_copy(taps_hbm, taps_ref, in_sem.at[chunks + 1]),
        pltpu.make_async_copy(w_hbm, w_ref, in_sem.at[chunks + 2]),
    ]
    loads = [pltpu.make_async_copy(halo_hbm, vb.at[:, pl.ds(0, lead)], in_sem.at[chunks])]
    for c in range(chunks):
        span = per * FFT
        loads.append(
            pltpu.make_async_copy(
                v_hbm.at[:, pl.ds(c * span, span)], vb.at[:, pl.ds(lead + c * span, span)], in_sem.at[c]
            )
        )
    for load in (table_loads[0], *loads, table_loads[1]):
        load.start()

    z = chan & 7
    y = (chan >> 4) & 3
    x = ((chan >> 3) & 1) * 2 + (blk >> 1)
    core = blk & 1

    def place(dx, dy, dz, dc):
        tx = (x + dx) & 3
        tc = (((y + dy) & 3) << 4) | ((tx >> 1) << 3) | ((z + dz) & 7)
        tb = ((tx & 1) << 1) | (core ^ dc)
        return tc, tb

    barrier = pltpu.get_barrier_semaphore()

    def greet(r, _):
        for dz in (4, 3, 5, 2, 6, 1, 7, 0):
            tc, tb = place((r & 3) ^ 2, ((r >> 2) & 3) ^ 2, dz, r >> 4)

            def signal():
                pl.semaphore_signal(barrier, inc=1, device_id=(tc, tb), device_id_type=MESH)

            if dz:
                signal()
            else:
                pl.when(r != 10)(signal)
        return 0

    lax.fori_loop(0, 32, greet, 0)

    def sample(f):
        return vb[:, pl.ds(pl.multiple_of(f * FFT, FFT), FFT)].astype(jnp.float32)

    table_loads[0].wait()
    taps = [taps_ref[pl.ds(t, 1), :] for t in range(TAPS)]

    def filter_frames(g, window):
        window = list(window)
        for u in range(4):
            f = g * 4 + u
            window.append(sample(f + HISTORY))
            value = taps[0] * window[0]
            for t in range(1, TAPS):
                value = value + taps[t] * window[t]
            window = window[1:]
            folded = (value[:, :HALF] + value[:, HALF:], value[:, :HALF] - value[:, HALF:])
            for parity in range(2):
                for lane in range(HALF // 128):
                    fold[parity * 2 + lane, pl.ds(f, inputs, stride=FOLD_PITCH), :] = folded[parity][
                        :, lane * 128 : (lane + 1) * 128
                    ]
        return tuple(window)

    loads[0].wait()
    window = tuple(sample(f) for f in range(HISTORY))
    for c in range(chunks):
        loads[c + 1].wait()
        window = lax.fori_loop(c * per // 4, (c + 1) * per // 4, filter_frames, window)

    def transform(slot, parity):
        def body(p, _):
            base = pl.multiple_of(p * 2 * FOLD_PITCH, 8)
            halves = []
            for lane in range(HALF // 128):
                source = fold.at[parity * 2 + lane]
                halves.append(
                    jnp.concatenate(
                        [source[pl.ds(base, frames), :], source[pl.ds(base + FOLD_PITCH, frames), :]], axis=0
                    )
                )
            value = jnp.concatenate(halves, axis=1)
            high = value.astype(jnp.bfloat16)
            low = (value - high.astype(jnp.float32)).astype(jnp.bfloat16)
            out = lax.dot_general(
                w_ref[parity],
                jnp.concatenate([high, low, high], axis=1),
                (((1,), (1,)), ((), ())),
                preferred_element_type=jnp.float32,
            )
            for h in range(2):
                for part in range(2):
                    turn[slot, pl.ds(part * inputs + p * 2 + h, NC // 2, stride=TURN_PITCH), :] = out[
                        part * NC // 2 : (part + 1) * NC // 2, h * frames : (h + 1) * frames
                    ]
            return 0

        lax.fori_loop(0, inputs // 2, body, 0)

    def pack(phase, slot, half):
        def body(g, _):
            for u in range(4):
                m = g * 4 + u
                start = (2 * m + half) * TURN_PITCH
                for part in range(2):
                    spec[phase, m, :, part * frames : (part + 1) * frames] = turn[
                        slot, pl.ds(start + part * inputs, inputs), :
                    ].astype(jnp.bfloat16)
            return 0

        lax.fori_loop(0, NC // 16, body, 0)

    row = pl.ds(pl.multiple_of(chan * inputs, inputs), inputs)

    def landing(phase):
        return last_ref if phase == 3 else landed.at[phase]

    def send(phase):
        shift_x, shift_core = phase & 1, phase >> 1
        if phase == 0:
            pltpu.make_async_copy(spec.at[0, chan], landing(0).at[row, :], recv_sem.at[0]).start()

        def body(r, _):
            for dz in (1, 7, 2, 6, 3, 5, 4, 0):
                tc, tb = place(shift_x + 2 * (r & 1), r >> 1, dz, shift_core)

                def copy():
                    pltpu.make_async_remote_copy(
                        src_ref=spec.at[phase, tc],
                        dst_ref=landing(phase).at[row, :],
                        send_sem=send_sem,
                        recv_sem=recv_sem.at[phase],
                        device_id=(tc, tb),
                        device_id_type=MESH,
                    ).start()

                if dz or phase:
                    copy()
                else:
                    pl.when(r > 0)(copy)
            return 0

        lax.fori_loop(0, 8, body, 0)

    table_loads[1].wait()
    for group in range(2):
        parity = core ^ group
        transform(group, parity)
        for shift_x in range(2):
            phase = group * 2 + shift_x
            pack(phase, group, (blk >> 1) ^ shift_x)
            if phase == 0:
                pl.semaphore_wait(barrier, 255)
            send(phase)

    def accumulate(phase):
        source = landed.at[phase]
        step = 256

        def body(r, _):
            rows = pl.ds(pl.multiple_of(r * step, step), step)
            left = source[rows, :]
            swapped = jnp.concatenate([left[:, frames:], -left[:, :frames]], axis=1)
            for operand, out in ((left, re_ref), (swapped, im_ref)):
                value = lax.dot_general(
                    operand, source[...], (((1,), (1,)), ((), ())), preferred_element_type=jnp.float32
                )
                if phase == 0:
                    out[rows, :] = value
                else:
                    out[rows, :] += value
            return 0

        lax.fori_loop(0, NI // step, body, 0)

    for phase in range(4):
        block = landing(phase)
        pltpu.make_async_copy(block, block, recv_sem.at[phase]).wait()
        if phase < 3:
            accumulate(phase)
    pltpu.make_async_copy(landed, landed, send_sem).wait()
    sent = spec.at[0, pl.ds(0, NC // 4 - 1)]
    pltpu.make_async_copy(sent, sent, send_sem).wait()


def exchange(voltages, halo, taps, weights):
    inputs, samples = voltages.shape
    frames = samples // FFT
    chunks = 4
    hbm = pl.BlockSpec(memory_space=pltpu.HBM)
    vmem = pl.BlockSpec(memory_space=pltpu.VMEM)
    square = jax.ShapeDtypeStruct((NI, NI), jnp.float32)
    return pl.pallas_call(
        functools.partial(exchange_kernel, frames),
        out_shape=(jax.ShapeDtypeStruct((NI, 2 * frames), jnp.bfloat16), square, square),
        in_specs=[hbm, hbm, hbm, hbm],
        out_specs=(vmem, vmem, vmem),
        scratch_shapes=[
            pltpu.VMEM((inputs, HISTORY * FFT + samples), jnp.int32),
            pltpu.VMEM(taps.shape, taps.dtype),
            pltpu.VMEM(weights.shape, weights.dtype),
            pltpu.VMEM((FFT // 128, inputs * FOLD_PITCH, 128), jnp.float32),
            pltpu.VMEM((2, NC // 2 * TURN_PITCH, frames), jnp.float32),
            pltpu.VMEM((4, NC // 4, inputs, 2 * frames), jnp.bfloat16),
            pltpu.VMEM((3, NI, 2 * frames), jnp.bfloat16),
            pltpu.SemaphoreType.DMA((chunks + 3,)),
            pltpu.SemaphoreType.DMA,
            pltpu.SemaphoreType.DMA((4,)),
        ],
        compiler_params=pltpu.CompilerParams(
            collective_id=0, has_side_effects=True, vmem_limit_bytes=44 * 1024 * 1024
        ),
        name="filterbank_exchange",
    )(voltages, halo, taps, weights)


def finish_kernel(frames, total, step, last_ref, re_in, im_in, re_ref, im_ref):
    rows = pl.ds(pl.multiple_of(pl.program_id(0) * step, step), step)
    left = last_ref[rows, :]
    swapped = jnp.concatenate([left[:, frames:], -left[:, :frames]], axis=1)
    for operand, partial, out in ((left, re_in, re_ref), (swapped, im_in, im_ref)):
        value = lax.dot_general(
            operand, last_ref[...], (((1,), (1,)), ((), ())), preferred_element_type=jnp.float32
        )
        out[0] = (partial[rows, :] + value) * (1.0 / total)


def finish(last, real, imag, frames):
    step = 128
    shape = jax.ShapeDtypeStruct((1, NI, NI), jnp.float32)
    out = pl.BlockSpec((1, step, NI), lambda i: (0, i, 0))
    vmem = pl.BlockSpec(memory_space=pltpu.VMEM)
    return pl.pallas_call(
        functools.partial(finish_kernel, frames, 4 * frames, step),
        out_shape=(shape, shape),
        grid=(NI // step,),
        in_specs=[vmem, vmem, vmem],
        out_specs=(out, out),
        compiler_params=pltpu.CompilerParams(vmem_limit_bytes=24 * 1024 * 1024),
        name="finish",
    )(last, real, imag)


def local(voltages):
    frames = voltages.shape[1] // FFT
    taps, weights = tables()
    tail = voltages[:, (frames - HISTORY) * FFT :]
    halo = shifted(tail, "blk", 1)
    last, real, imag = exchange(voltages, halo, jnp.asarray(taps), jnp.asarray(weights))
    return finish(last, real, imag, frames)


def solution(mesh):
    return jax.shard_map(
        local,
        mesh=mesh,
        in_specs=(P("chan", "blk"),),
        out_specs=(P(("chan", "blk"), None, None), P(("chan", "blk"), None, None)),
        check_vma=False,
    )
```

```python
import functools

import jax
import jax.numpy as jnp
import numpy as np
from jax import lax
from jax.experimental import pallas as pl
from jax.experimental.pallas import tpu as pltpu
from jax.sharding import PartitionSpec as P

NI = 1024
NC = 256
TAPS = 4
FFT = 512
HALF = FFT // 2
HISTORY = TAPS - 1
MESH = pl.DeviceIdType.MESH


def tables():
    length = TAPS * FFT
    points = np.arange(length, dtype=np.float64)
    window = 0.54 - 0.46 * np.cos(2.0 * np.pi * points / (length - 1))
    taps = (np.sinc((points - (length - 1) / 2.0) / FFT) * window).reshape(TAPS, FFT)
    scale = 1.0 / (56.0 * np.sqrt(FFT * np.mean(np.sum(taps * taps, axis=0))))
    weights = []
    for parity in range(2):
        channel = np.arange(parity, NC, 2)[:, None]
        angle = (channel * np.arange(HALF)[None, :] % FFT) * (2.0 * np.pi / FFT)
        weights.append(scale * np.concatenate([np.cos(angle), -np.sin(angle)], axis=0))
    return np.concatenate([*weights, taps.reshape(2 * TAPS, HALF)], axis=0).astype(np.float32)


FOLD_PITCH = 132
TURN_PITCH = 36
EARLY = 2


def exchange_kernel(
    frames,
    v_hbm,
    table_hbm,
    last_ref,
    re_ref,
    im_ref,
    vb,
    table,
    w_ref,
    tail,
    tail_out,
    halo,
    fold,
    head,
    turn,
    extra,
    spec,
    landed,
    in_sem,
    halo_sem,
    send_sem,
    recv_sem,
):
    inputs = v_hbm.shape[0]
    chan = lax.axis_index("chan")
    blk = lax.axis_index("blk")
    blocks = lax.axis_size("blk")
    chunks = in_sem.shape[0] - 2
    per = frames // chunks
    lead = HISTORY * FFT
    table_load = pltpu.make_async_copy(table_hbm, table, in_sem.at[chunks])
    tail_load = pltpu.make_async_copy(v_hbm.at[:, pl.ds(frames * FFT - lead, lead)], tail, in_sem.at[chunks + 1])
    loads = []
    for c in range(chunks):
        span = pl.ds(c * per * FFT, per * FFT)
        loads.append(pltpu.make_async_copy(v_hbm.at[:, span], vb.at[:, span], in_sem.at[c]))
    for load in (table_load, *loads, tail_load):
        load.start()

    z = chan & 7
    y = (chan >> 4) & 3
    x = ((chan >> 3) & 1) * 2 + (blk >> 1)
    core = blk & 1
    along = [(z + dz) & 7 for dz in range(8)]

    def place(dx, dy, dc):
        tx = (x + dx) & 3
        return (((y + dy) & 3) << 4) | ((tx >> 1) << 3), ((tx & 1) << 1) | (core ^ dc)

    barrier = pltpu.get_barrier_semaphore()

    def greet(r, _):
        base, tb = place((r & 3) ^ 2, ((r >> 2) & 3) ^ 2, r >> 4)
        for dz in (4, 3, 5, 2, 6, 1, 7, 0):

            def signal():
                pl.semaphore_signal(barrier, inc=1, device_id=(base | along[dz], tb), device_id_type=MESH)

            if dz:
                signal()
            else:
                pl.when(r != 10)(signal)
        return 0

    lax.fori_loop(0, 32, greet, 0)

    head[...] = jnp.zeros_like(head)
    table_load.wait()
    for parity in range(2):
        value = table[pl.ds(parity * 2 * (NC // 2), NC), :]
        high = value.astype(jnp.bfloat16)
        w_ref[parity, 0:NC, :] = high
        w_ref[parity, NC : 2 * NC, :] = (value - high.astype(jnp.float32)).astype(jnp.bfloat16)

    def tap(t):
        row = 2 * NC + 2 * t
        return jnp.concatenate([table[row : row + 1, :], table[row + 1 : row + 2, :]], axis=1)

    taps = [tap(t) for t in range(TAPS)]

    def place_frame(ref, f, pitch, value):
        folded = (value[:, :HALF] + value[:, HALF:], value[:, :HALF] - value[:, HALF:])
        for parity in range(2):
            for lane in range(HALF // 128):
                ref[parity * 2 + lane, pl.ds(f, inputs, stride=pitch), :] = folded[parity][
                    :, lane * 128 : (lane + 1) * 128
                ]

    def filter_frames(g, window):
        window = list(window)
        for u in range(4):
            f = g * 4 + u
            window.append(vb[:, pl.ds(pl.multiple_of(f * FFT, FFT), FFT)].astype(jnp.float32))
            value = taps[0] * window[0]
            for t in range(1, TAPS):
                value = value + taps[t] * window[t]
            window = window[1:]
            place_frame(fold, f, FOLD_PITCH, value)
        return tuple(window)

    window = tuple(jnp.zeros((inputs, FFT), jnp.float32) for _ in range(HISTORY))
    for c in range(chunks):
        loads[c].wait()
        window = lax.fori_loop(c * per // 4, (c + 1) * per // 4, filter_frames, window)

    def spectra(parity, value):
        high = value.astype(jnp.bfloat16)
        low = (value - high.astype(jnp.float32)).astype(jnp.bfloat16)
        contract = (((1,), (1,)), ((), ()))
        both = lax.dot_general(w_ref[parity], high, contract, preferred_element_type=jnp.float32)
        rest = lax.dot_general(w_ref[parity, 0:NC, :], low, contract, preferred_element_type=jnp.float32)
        return both[0:NC] + (both[NC : 2 * NC] + rest)

    def transform(slot, parity, first, last):
        def body(p, _):
            base = pl.multiple_of(p * 2 * FOLD_PITCH, 8)
            halves = []
            for lane in range(HALF // 128):
                source = fold.at[parity * 2 + lane]
                halves.append(
                    jnp.concatenate(
                        [source[pl.ds(base, frames), :], source[pl.ds(base + FOLD_PITCH, frames), :]], axis=0
                    )
                )
            out = spectra(parity, jnp.concatenate(halves, axis=1))
            for h in range(2):
                for part in range(2):
                    turn[slot, pl.ds(part * inputs + p * 2 + h, NC // 2, stride=TURN_PITCH), :] = out[
                        part * NC // 2 : (part + 1) * NC // 2, h * frames : (h + 1) * frames
                    ]
            return 0

        lax.fori_loop(first, last, body, 0)

    slots = head.shape[1] // inputs

    def patch(parity):
        out = spectra(parity, jnp.concatenate([head[parity * 2], head[parity * 2 + 1]], axis=1))
        for i in range(inputs):
            for part in range(2):
                value = out[part * NC // 2 : (part + 1) * NC // 2, :]
                if i:
                    value = pltpu.roll(value, 128 - slots * i, 1)
                extra[pl.ds(part * inputs + i, NC // 2, stride=TURN_PITCH), :] = value

    first_lanes = lax.broadcasted_iota(jnp.int32, (inputs, frames), 1) < slots

    def pack(phase, slot, half):
        def body(g, _):
            for u in range(4):
                m = g * 4 + u
                start = (2 * m + half) * TURN_PITCH
                for part in range(2):
                    rows = pl.ds(start + part * inputs, inputs)
                    value = turn[slot, rows, :] + jnp.where(first_lanes, extra[rows, :], 0.0)
                    spec[phase, m, :, part * frames : (part + 1) * frames] = value.astype(jnp.bfloat16)
            return 0

        lax.fori_loop(0, NC // 16, body, 0)

    row = pl.ds(pl.multiple_of(chan * inputs, inputs), inputs)

    def landing(phase):
        return last_ref if phase == 3 else landed.at[phase]

    def send(phase):
        shift_x, shift_core = phase & 1, phase >> 1
        if phase == 0:
            pltpu.make_async_copy(spec.at[0, chan], landing(0).at[row, :], recv_sem.at[0]).start()

        def body(r, _):
            base, tb = place(shift_x + 2 * (r & 1), r >> 1, shift_core)
            for dz in (1, 7, 2, 6, 3, 5, 4, 0):
                tc = base | along[dz]

                def copy():
                    pltpu.make_async_remote_copy(
                        src_ref=spec.at[phase, tc],
                        dst_ref=landing(phase).at[row, :],
                        send_sem=send_sem,
                        recv_sem=recv_sem.at[phase],
                        device_id=(tc, tb),
                        device_id_type=MESH,
                    ).start()

                if dz or phase:
                    copy()
                else:
                    pl.when(r > 0)(copy)
            return 0

        lax.fori_loop(0, 8, body, 0)

    tail_load.wait()
    tail_out[...] = tail[...].astype(jnp.bfloat16)
    pairs = inputs // 2
    transform(0, core, 0, pairs // 2)
    pl.semaphore_wait(barrier, 255)
    onward = pltpu.make_async_remote_copy(
        src_ref=tail_out,
        dst_ref=halo,
        send_sem=halo_sem.at[0],
        recv_sem=halo_sem.at[1],
        device_id=(chan, jnp.minimum(blk + 1, blocks - 1)),
        device_id_type=MESH,
    )

    @pl.when(blk < blocks - 1)
    def _():
        onward.start()

    transform(0, core, pairs // 2, pairs)
    transform(1, core ^ 1, 0, EARLY)

    @pl.when(blk > 0)
    def _():
        onward.wait_recv()
        for f in range(HISTORY):
            value = None
            for t in range(HISTORY - f):
                earlier = halo[:, (f + t) * FFT : (f + t + 1) * FFT].astype(jnp.float32)
                value = taps[t] * earlier if value is None else value + taps[t] * earlier
            place_frame(head, f, slots, value)

    for group in range(2):
        if group:
            transform(1, core ^ 1, EARLY, pairs)
        patch(core ^ group)
        for shift_x in range(2):
            phase = group * 2 + shift_x
            pack(phase, group, (blk >> 1) ^ shift_x)
            send(phase)

    @pl.when(blk < blocks - 1)
    def _():
        onward.wait_send()

    def accumulate(phase):
        source = landed.at[phase]
        step = 256

        def body(r, _):
            rows = pl.ds(pl.multiple_of(r * step, step), step)
            left = source[rows, :]
            swapped = jnp.concatenate([left[:, frames:], -left[:, :frames]], axis=1)
            for operand, out in ((left, re_ref), (swapped, im_ref)):
                value = lax.dot_general(
                    operand, source[...], (((1,), (1,)), ((), ())), preferred_element_type=jnp.float32
                )
                if phase == 0:
                    out[rows, :] = value
                else:
                    out[rows, :] += value
            return 0

        lax.fori_loop(0, NI // step, body, 0)

    for phase in range(4):
        block = landing(phase)
        pltpu.make_async_copy(block, block, recv_sem.at[phase]).wait()
        if phase < 3:
            accumulate(phase)
    pltpu.make_async_copy(landed, landed, send_sem).wait()
    sent = spec.at[0, pl.ds(0, NC // 4 - 1)]
    pltpu.make_async_copy(sent, sent, send_sem).wait()


def exchange(voltages, table):
    inputs, samples = voltages.shape
    frames = samples // FFT
    chunks = 4
    hbm = pl.BlockSpec(memory_space=pltpu.HBM)
    vmem = pl.BlockSpec(memory_space=pltpu.VMEM)
    square = jax.ShapeDtypeStruct((NI, NI), jnp.float32)
    return pl.pallas_call(
        functools.partial(exchange_kernel, frames),
        out_shape=(jax.ShapeDtypeStruct((NI, 2 * frames), jnp.bfloat16), square, square),
        in_specs=[hbm, hbm],
        out_specs=(vmem, vmem, vmem),
        scratch_shapes=[
            pltpu.VMEM((inputs, samples), jnp.int32),
            pltpu.VMEM(table.shape, jnp.float32),
            pltpu.VMEM((2, 2 * NC, HALF), jnp.bfloat16),
            pltpu.VMEM((inputs, HISTORY * FFT), jnp.int32),
            pltpu.VMEM((inputs, HISTORY * FFT), jnp.bfloat16),
            pltpu.VMEM((inputs, HISTORY * FFT), jnp.bfloat16),
            pltpu.VMEM((FFT // 128, inputs * FOLD_PITCH, 128), jnp.float32),
            pltpu.VMEM((FFT // 128, 128, 128), jnp.float32),
            pltpu.VMEM((2, NC // 2 * TURN_PITCH, frames), jnp.float32),
            pltpu.VMEM((NC // 2 * TURN_PITCH, frames), jnp.float32),
            pltpu.VMEM((4, NC // 4, inputs, 2 * frames), jnp.bfloat16),
            pltpu.VMEM((3, NI, 2 * frames), jnp.bfloat16),
            pltpu.SemaphoreType.DMA((chunks + 2,)),
            pltpu.SemaphoreType.DMA((2,)),
            pltpu.SemaphoreType.DMA,
            pltpu.SemaphoreType.DMA((4,)),
        ],
        compiler_params=pltpu.CompilerParams(
            collective_id=0, has_side_effects=True, vmem_limit_bytes=44 * 1024 * 1024
        ),
        name="filterbank_exchange",
    )(voltages, table)


def finish_kernel(frames, total, step, last_ref, re_in, im_in, re_ref, im_ref):
    rows = pl.ds(pl.multiple_of(pl.program_id(0) * step, step), step)
    left = last_ref[rows, :]
    swapped = jnp.concatenate([left[:, frames:], -left[:, :frames]], axis=1)
    for operand, partial, out in ((left, re_in, re_ref), (swapped, im_in, im_ref)):
        value = lax.dot_general(
            operand, last_ref[...], (((1,), (1,)), ((), ())), preferred_element_type=jnp.float32
        )
        out[0] = (partial[rows, :] + value) * (1.0 / total)


def finish(last, real, imag, frames):
    step = 256
    shape = jax.ShapeDtypeStruct((1, NI, NI), jnp.float32)
    out = pl.BlockSpec((1, step, NI), lambda i: (0, i, 0))
    vmem = pl.BlockSpec(memory_space=pltpu.VMEM)
    return pl.pallas_call(
        functools.partial(finish_kernel, frames, 4 * frames, step),
        out_shape=(shape, shape),
        grid=(NI // step,),
        in_specs=[vmem, vmem, vmem],
        out_specs=(out, out),
        compiler_params=pltpu.CompilerParams(vmem_limit_bytes=24 * 1024 * 1024),
        name="finish",
    )(last, real, imag)


def local(voltages):
    frames = voltages.shape[1] // FFT
    last, real, imag = exchange(voltages, pltpu.with_memory_space_constraint(jnp.asarray(tables()), pltpu.HBM))
    return finish(last, real, imag, frames)


def solution(mesh):
    return jax.shard_map(
        local,
        mesh=mesh,
        in_specs=(P("chan", "blk"),),
        out_specs=(P(("chan", "blk"), None, None), P(("chan", "blk"), None, None)),
        check_vma=False,
    )
```

```python
import functools

import jax
import jax.numpy as jnp
import numpy as np
from jax import lax
from jax.experimental import pallas as pl
from jax.experimental.pallas import tpu as pltpu
from jax.sharding import PartitionSpec as P

NI = 1024
NC = 256
TAPS = 4
FFT = 512
HALF = FFT // 2
HISTORY = TAPS - 1
MESH = pl.DeviceIdType.MESH


def tables():
    length = TAPS * FFT
    points = np.arange(length, dtype=np.float64)
    window = 0.54 - 0.46 * np.cos(2.0 * np.pi * points / (length - 1))
    taps = (np.sinc((points - (length - 1) / 2.0) / FFT) * window).reshape(TAPS, FFT)
    scale = 1.0 / (56.0 * np.sqrt(FFT * np.mean(np.sum(taps * taps, axis=0))))
    weights = []
    for parity in range(2):
        channel = np.arange(parity, NC, 2)[:, None]
        angle = (channel * np.arange(HALF)[None, :] % FFT) * (2.0 * np.pi / FFT)
        weights.append(scale * np.concatenate([np.cos(angle), -np.sin(angle)], axis=0))
    return np.concatenate([*weights, taps.reshape(2 * TAPS, HALF)], axis=0).astype(np.float32)


FOLD_PITCH = 132
TURN_PITCH = 36
EARLY = 2


def exchange_kernel(
    frames,
    v_hbm,
    table_hbm,
    last_ref,
    re_ref,
    im_ref,
    vb,
    table,
    w_ref,
    tail,
    tail_out,
    halo,
    fold,
    head,
    turn,
    extra,
    spec,
    landed,
    in_sem,
    halo_sem,
    plane_sem,
    send_sem,
    recv_sem,
):
    inputs = v_hbm.shape[0]
    chan = lax.axis_index("chan")
    blk = lax.axis_index("blk")
    blocks = lax.axis_size("blk")
    chunks = in_sem.shape[0] - 2
    per = frames // chunks
    lead = HISTORY * FFT
    table_load = pltpu.make_async_copy(table_hbm, table, in_sem.at[chunks])
    tail_load = pltpu.make_async_copy(v_hbm.at[:, pl.ds(frames * FFT - lead, lead)], tail, in_sem.at[chunks + 1])
    loads = []
    for c in range(chunks):
        span = pl.ds(c * per * FFT, per * FFT)
        loads.append(pltpu.make_async_copy(v_hbm.at[:, span], vb.at[:, span], in_sem.at[c]))
    for load in (table_load, *loads, tail_load):
        load.start()

    z = chan & 7
    y = (chan >> 4) & 3
    x = ((chan >> 3) & 1) * 2 + (blk >> 1)
    core = blk & 1
    along = [(z + dz) & 7 for dz in range(8)]

    def place(dx, dy, dc):
        tx = (x + dx) & 3
        return (((y + dy) & 3) << 4) | ((tx >> 1) << 3), ((tx & 1) << 1) | (core ^ dc)

    barrier = pltpu.get_barrier_semaphore()

    mine = chan & ~7

    def signal(semaphore, tc, tb):
        pl.semaphore_signal(semaphore, inc=1, device_id=(tc, tb), device_id_type=MESH)

    for dz in (4, 3, 5, 2, 6, 1, 7):
        signal(barrier, mine | along[dz], blk)

    def greet(r, _):
        base, tb = place(r & 3, (r >> 2) & 3, r >> 4)
        signal(barrier, base | z, tb)
        return 0

    lax.fori_loop(1, 32, greet, 0)

    head[...] = jnp.zeros_like(head)
    table_load.wait()
    for parity in range(2):
        value = table[pl.ds(parity * 2 * (NC // 2), NC), :]
        high = value.astype(jnp.bfloat16)
        w_ref[parity, 0:NC, :] = high
        w_ref[parity, NC : 2 * NC, :] = (value - high.astype(jnp.float32)).astype(jnp.bfloat16)

    def tap(t):
        row = 2 * NC + 2 * t
        return jnp.concatenate([table[row : row + 1, :], table[row + 1 : row + 2, :]], axis=1)

    taps = [tap(t) for t in range(TAPS)]

    def place_frame(ref, f, pitch, value):
        folded = (value[:, :HALF] + value[:, HALF:], value[:, :HALF] - value[:, HALF:])
        for parity in range(2):
            for lane in range(HALF // 128):
                ref[parity * 2 + lane, pl.ds(f, inputs, stride=pitch), :] = folded[parity][
                    :, lane * 128 : (lane + 1) * 128
                ]

    def filter_frames(g, window):
        window = list(window)
        for u in range(4):
            f = g * 4 + u
            window.append(vb[:, pl.ds(pl.multiple_of(f * FFT, FFT), FFT)].astype(jnp.float32))
            value = taps[0] * window[0]
            for t in range(1, TAPS):
                value = value + taps[t] * window[t]
            window = window[1:]
            place_frame(fold, f, FOLD_PITCH, value)
        return tuple(window)

    window = tuple(jnp.zeros((inputs, FFT), jnp.float32) for _ in range(HISTORY))
    for c in range(chunks):
        loads[c].wait()
        window = lax.fori_loop(c * per // 4, (c + 1) * per // 4, filter_frames, window)

    def spectra(parity, value):
        high = value.astype(jnp.bfloat16)
        low = (value - high.astype(jnp.float32)).astype(jnp.bfloat16)
        contract = (((1,), (1,)), ((), ()))
        both = lax.dot_general(w_ref[parity], high, contract, preferred_element_type=jnp.float32)
        rest = lax.dot_general(w_ref[parity, 0:NC, :], low, contract, preferred_element_type=jnp.float32)
        return both[0:NC] + (both[NC : 2 * NC] + rest)

    def transform(slot, parity, first, last):
        def body(p, _):
            base = pl.multiple_of(p * 2 * FOLD_PITCH, 8)
            halves = []
            for lane in range(HALF // 128):
                source = fold.at[parity * 2 + lane]
                halves.append(
                    jnp.concatenate(
                        [source[pl.ds(base, frames), :], source[pl.ds(base + FOLD_PITCH, frames), :]], axis=0
                    )
                )
            out = spectra(parity, jnp.concatenate(halves, axis=1))
            for h in range(2):
                for part in range(2):
                    turn[slot, pl.ds(part * inputs + p * 2 + h, NC // 2, stride=TURN_PITCH), :] = out[
                        part * NC // 2 : (part + 1) * NC // 2, h * frames : (h + 1) * frames
                    ]
            return 0

        lax.fori_loop(first, last, body, 0)

    slots = head.shape[1] // inputs

    def patch(parity):
        out = spectra(parity, jnp.concatenate([head[parity * 2], head[parity * 2 + 1]], axis=1))
        for i in range(inputs):
            for part in range(2):
                value = out[part * NC // 2 : (part + 1) * NC // 2, :]
                if i:
                    value = pltpu.roll(value, 128 - slots * i, 1)
                extra[pl.ds(part * inputs + i, NC // 2, stride=TURN_PITCH), :] = value

    first_lanes = lax.broadcasted_iota(jnp.int32, (inputs, frames), 1) < slots

    def pack(phase, slot, half):
        def body(g, _):
            for u in range(4):
                m = g * 4 + u
                start = (2 * m + half) * TURN_PITCH
                for part in range(2):
                    rows = pl.ds(start + part * inputs, inputs)
                    value = turn[slot, rows, :] + jnp.where(first_lanes, extra[rows, :], 0.0)
                    spec[phase, m, :, part * frames : (part + 1) * frames] = value.astype(jnp.bfloat16)
            return 0

        lax.fori_loop(0, NC // 16, body, 0)

    row = pl.ds(pl.multiple_of(chan * inputs, inputs), inputs)

    def landing(phase):
        return last_ref if phase == 3 else landed.at[phase]

    def send(phase):
        shift_x, shift_core = phase & 1, phase >> 1
        if phase == 0:
            pltpu.make_async_copy(spec.at[0, chan], landing(0).at[row, :], recv_sem.at[0]).start()

        def body(r, _):
            base, tb = place(shift_x + 2 * (r & 1), r >> 1, shift_core)
            for dz in (1, 7, 2, 6, 3, 5, 4, 0):
                tc = base | along[dz]

                def copy():
                    pltpu.make_async_remote_copy(
                        src_ref=spec.at[phase, tc],
                        dst_ref=landing(phase).at[row, :],
                        send_sem=send_sem,
                        recv_sem=recv_sem.at[phase],
                        device_id=(tc, tb),
                        device_id_type=MESH,
                    ).start()

                if dz or phase:
                    copy()
                else:
                    pl.when(r > 0)(copy)
            return 0

        lax.fori_loop(0, 8, body, 0)

    tail_load.wait()
    tail_out[...] = tail[...].astype(jnp.bfloat16)
    pairs = inputs // 2
    transform(0, core, 0, pairs // 2)
    pl.semaphore_wait(barrier, 38)
    for dz in (4, 3, 5, 2, 6, 1, 7):
        signal(plane_sem, mine | along[dz], blk)
    onward = pltpu.make_async_remote_copy(
        src_ref=tail_out,
        dst_ref=halo,
        send_sem=halo_sem.at[0],
        recv_sem=halo_sem.at[1],
        device_id=(chan, jnp.minimum(blk + 1, blocks - 1)),
        device_id_type=MESH,
    )

    @pl.when(blk < blocks - 1)
    def _():
        onward.start()

    transform(0, core, pairs // 2, pairs)
    transform(1, core ^ 1, 0, EARLY)

    @pl.when(blk > 0)
    def _():
        onward.wait_recv()
        for f in range(HISTORY):
            value = None
            for t in range(HISTORY - f):
                earlier = halo[:, (f + t) * FFT : (f + t + 1) * FFT].astype(jnp.float32)
                value = taps[t] * earlier if value is None else value + taps[t] * earlier
            place_frame(head, f, slots, value)

    for group in range(2):
        if group:
            transform(1, core ^ 1, EARLY, pairs)
        patch(core ^ group)
        for shift_x in range(2):
            phase = group * 2 + shift_x
            pack(phase, group, (blk >> 1) ^ shift_x)
            if phase == 0:
                pl.semaphore_wait(plane_sem, 7)
            send(phase)

    @pl.when(blk < blocks - 1)
    def _():
        onward.wait_send()

    def accumulate(phase):
        source = landed.at[phase]
        step = 256

        def body(r, _):
            rows = pl.ds(pl.multiple_of(r * step, step), step)
            left = source[rows, :]
            swapped = jnp.concatenate([left[:, frames:], -left[:, :frames]], axis=1)
            for operand, out in ((left, re_ref), (swapped, im_ref)):
                value = lax.dot_general(
                    operand, source[...], (((1,), (1,)), ((), ())), preferred_element_type=jnp.float32
                )
                if phase == 0:
                    out[rows, :] = value
                else:
                    out[rows, :] += value
            return 0

        lax.fori_loop(0, NI // step, body, 0)

    for phase in range(4):
        block = landing(phase)
        pltpu.make_async_copy(block, block, recv_sem.at[phase]).wait()
        if phase < 3:
            accumulate(phase)
    pltpu.make_async_copy(landed, landed, send_sem).wait()
    sent = spec.at[0, pl.ds(0, NC // 4 - 1)]
    pltpu.make_async_copy(sent, sent, send_sem).wait()


def exchange(voltages, table):
    inputs, samples = voltages.shape
    frames = samples // FFT
    chunks = 4
    hbm = pl.BlockSpec(memory_space=pltpu.HBM)
    vmem = pl.BlockSpec(memory_space=pltpu.VMEM)
    square = jax.ShapeDtypeStruct((NI, NI), jnp.float32)
    return pl.pallas_call(
        functools.partial(exchange_kernel, frames),
        out_shape=(jax.ShapeDtypeStruct((NI, 2 * frames), jnp.bfloat16), square, square),
        in_specs=[hbm, hbm],
        out_specs=(vmem, vmem, vmem),
        scratch_shapes=[
            pltpu.VMEM((inputs, samples), jnp.int32),
            pltpu.VMEM(table.shape, jnp.float32),
            pltpu.VMEM((2, 2 * NC, HALF), jnp.bfloat16),
            pltpu.VMEM((inputs, HISTORY * FFT), jnp.int32),
            pltpu.VMEM((inputs, HISTORY * FFT), jnp.bfloat16),
            pltpu.VMEM((inputs, HISTORY * FFT), jnp.bfloat16),
            pltpu.VMEM((FFT // 128, inputs * FOLD_PITCH, 128), jnp.float32),
            pltpu.VMEM((FFT // 128, 128, 128), jnp.float32),
            pltpu.VMEM((2, NC // 2 * TURN_PITCH, frames), jnp.float32),
            pltpu.VMEM((NC // 2 * TURN_PITCH, frames), jnp.float32),
            pltpu.VMEM((4, NC // 4, inputs, 2 * frames), jnp.bfloat16),
            pltpu.VMEM((3, NI, 2 * frames), jnp.bfloat16),
            pltpu.SemaphoreType.DMA((chunks + 2,)),
            pltpu.SemaphoreType.DMA((2,)),
            pltpu.SemaphoreType.REGULAR,
            pltpu.SemaphoreType.DMA,
            pltpu.SemaphoreType.DMA((4,)),
        ],
        compiler_params=pltpu.CompilerParams(
            collective_id=0, has_side_effects=True, vmem_limit_bytes=44 * 1024 * 1024
        ),
        name="filterbank_exchange",
    )(voltages, table)


def finish_kernel(frames, total, step, last_ref, re_in, im_in, re_ref, im_ref):
    rows = pl.ds(pl.multiple_of(pl.program_id(0) * step, step), step)
    left = last_ref[rows, :]
    swapped = jnp.concatenate([left[:, frames:], -left[:, :frames]], axis=1)
    for operand, partial, out in ((left, re_in, re_ref), (swapped, im_in, im_ref)):
        value = lax.dot_general(
            operand, last_ref[...], (((1,), (1,)), ((), ())), preferred_element_type=jnp.float32
        )
        out[0] = (partial[rows, :] + value) * (1.0 / total)


def finish(last, real, imag, frames):
    step = 256
    shape = jax.ShapeDtypeStruct((1, NI, NI), jnp.float32)
    out = pl.BlockSpec((1, step, NI), lambda i: (0, i, 0))
    vmem = pl.BlockSpec(memory_space=pltpu.VMEM)
    return pl.pallas_call(
        functools.partial(finish_kernel, frames, 4 * frames, step),
        out_shape=(shape, shape),
        grid=(NI // step,),
        in_specs=[vmem, vmem, vmem],
        out_specs=(out, out),
        compiler_params=pltpu.CompilerParams(vmem_limit_bytes=24 * 1024 * 1024),
        name="finish",
    )(last, real, imag)


def local(voltages):
    frames = voltages.shape[1] // FFT
    last, real, imag = exchange(voltages, pltpu.with_memory_space_constraint(jnp.asarray(tables()), pltpu.HBM))
    return finish(last, real, imag, frames)


def solution(mesh):
    return jax.shard_map(
        local,
        mesh=mesh,
        in_specs=(P("chan", "blk"),),
        out_specs=(P(("chan", "blk"), None, None), P(("chan", "blk"), None, None)),
        check_vma=False,
    )
```

```python
import functools

import jax
import jax.numpy as jnp
import numpy as np
from jax import lax
from jax.experimental import pallas as pl
from jax.experimental.pallas import tpu as pltpu
from jax.sharding import PartitionSpec as P

NI = 1024
NC = 256
TAPS = 4
FFT = 512
HALF = FFT // 2
HISTORY = TAPS - 1
MESH = pl.DeviceIdType.MESH


def tables():
    length = TAPS * FFT
    points = np.arange(length, dtype=np.float64)
    window = 0.54 - 0.46 * np.cos(2.0 * np.pi * points / (length - 1))
    taps = (np.sinc((points - (length - 1) / 2.0) / FFT) * window).reshape(TAPS, FFT)
    scale = 1.0 / (56.0 * np.sqrt(FFT * np.mean(np.sum(taps * taps, axis=0))))
    weights = []
    for parity in range(2):
        channel = np.arange(parity, NC, 2)[:, None]
        angle = (channel * np.arange(HALF)[None, :] % FFT) * (2.0 * np.pi / FFT)
        weights.append(scale * np.concatenate([np.cos(angle), -np.sin(angle)], axis=0))
    return np.concatenate([*weights, taps.reshape(2 * TAPS, HALF)], axis=0).astype(np.float32)


FOLD_PITCH = 132
TURN_PITCH = 36
EARLY = 2


def exchange_kernel(
    frames,
    v_hbm,
    table_hbm,
    last_ref,
    re_ref,
    im_ref,
    vb,
    table,
    w_ref,
    tail,
    tail_out,
    halo,
    fold,
    head,
    turn,
    extra,
    spec,
    landed,
    in_sem,
    halo_sem,
    plane_sem,
    send_sem,
    recv_sem,
):
    inputs = v_hbm.shape[0]
    chan = lax.axis_index("chan")
    blk = lax.axis_index("blk")
    blocks = lax.axis_size("blk")
    chunks = in_sem.shape[0] - 2
    per = frames // chunks
    lead = HISTORY * FFT
    table_load = pltpu.make_async_copy(table_hbm, table, in_sem.at[chunks])
    tail_load = pltpu.make_async_copy(v_hbm.at[:, pl.ds(frames * FFT - lead, lead)], tail, in_sem.at[chunks + 1])
    loads = []
    for c in range(chunks):
        span = pl.ds(c * per * FFT, per * FFT)
        loads.append(pltpu.make_async_copy(v_hbm.at[:, span], vb.at[:, span], in_sem.at[c]))
    for load in (table_load, *loads, tail_load):
        load.start()

    z = chan & 7
    y = (chan >> 4) & 3
    x = ((chan >> 3) & 1) * 2 + (blk >> 1)
    core = blk & 1
    along = [(z + dz) & 7 for dz in range(8)]

    def place(dx, dy, dc):
        tx = (x + dx) & 3
        return (((y + dy) & 3) << 4) | ((tx >> 1) << 3), ((tx & 1) << 1) | (core ^ dc)

    barrier = pltpu.get_barrier_semaphore()

    mine = chan & ~7

    def signal(semaphore, tc, tb):
        pl.semaphore_signal(semaphore, inc=1, device_id=(tc, tb), device_id_type=MESH)

    for dz in (4, 3, 5, 2, 6, 1, 7):
        signal(barrier, mine | along[dz], blk)

    def greet(r, _):
        base, tb = place(r & 3, (r >> 2) & 3, r >> 4)
        signal(barrier, base | z, tb)
        return 0

    lax.fori_loop(1, 32, greet, 0)

    head[...] = jnp.zeros_like(head)
    table_load.wait()
    for parity in range(2):
        value = table[pl.ds(parity * 2 * (NC // 2), NC), :]
        high = value.astype(jnp.bfloat16)
        w_ref[parity, 0:NC, :] = high
        w_ref[parity, NC : 2 * NC, :] = (value - high.astype(jnp.float32)).astype(jnp.bfloat16)

    def tap(t):
        row = 2 * NC + 2 * t
        return jnp.concatenate([table[row : row + 1, :], table[row + 1 : row + 2, :]], axis=1)

    taps = [tap(t) for t in range(TAPS)]

    def place_frame(ref, f, pitch, value):
        folded = (value[:, :HALF] + value[:, HALF:], value[:, :HALF] - value[:, HALF:])
        for parity in range(2):
            for lane in range(HALF // 128):
                ref[parity * 2 + lane, pl.ds(f, inputs, stride=pitch), :] = folded[parity][
                    :, lane * 128 : (lane + 1) * 128
                ]

    def filter_frames(g, window):
        window = list(window)
        for u in range(4):
            f = g * 4 + u
            window.append(vb[:, pl.ds(pl.multiple_of(f * FFT, FFT), FFT)].astype(jnp.float32))
            value = taps[0] * window[0]
            for t in range(1, TAPS):
                value = value + taps[t] * window[t]
            window = window[1:]
            place_frame(fold, f, FOLD_PITCH, value)
        return tuple(window)

    window = tuple(jnp.zeros((inputs, FFT), jnp.float32) for _ in range(HISTORY))
    for c in range(chunks):
        loads[c].wait()
        window = lax.fori_loop(c * per // 4, (c + 1) * per // 4, filter_frames, window)

    def spectra(parity, value):
        high = value.astype(jnp.bfloat16)
        low = (value - high.astype(jnp.float32)).astype(jnp.bfloat16)
        contract = (((1,), (1,)), ((), ()))
        both = lax.dot_general(w_ref[parity], high, contract, preferred_element_type=jnp.float32)
        rest = lax.dot_general(w_ref[parity, 0:NC, :], low, contract, preferred_element_type=jnp.float32)
        return both[0:NC] + (both[NC : 2 * NC] + rest)

    def transform(slot, parity, first, last):
        def body(p, _):
            base = pl.multiple_of(p * 2 * FOLD_PITCH, 8)
            halves = []
            for lane in range(HALF // 128):
                source = fold.at[parity * 2 + lane]
                halves.append(
                    jnp.concatenate(
                        [source[pl.ds(base, frames), :], source[pl.ds(base + FOLD_PITCH, frames), :]], axis=0
                    )
                )
            out = spectra(parity, jnp.concatenate(halves, axis=1))
            for h in range(2):
                for part in range(2):
                    turn[slot, pl.ds(part * inputs + p * 2 + h, NC // 2, stride=TURN_PITCH), :] = out[
                        part * NC // 2 : (part + 1) * NC // 2, h * frames : (h + 1) * frames
                    ]
            return 0

        lax.fori_loop(first, last, body, 0)

    slots = head.shape[1] // inputs

    def patch(parity):
        out = spectra(parity, jnp.concatenate([head[parity * 2], head[parity * 2 + 1]], axis=1))
        for i in range(inputs):
            for part in range(2):
                value = out[part * NC // 2 : (part + 1) * NC // 2, :]
                if i:
                    value = pltpu.roll(value, 128 - slots * i, 1)
                extra[pl.ds(part * inputs + i, NC // 2, stride=TURN_PITCH), :] = value

    first_lanes = lax.broadcasted_iota(jnp.int32, (inputs, frames), 1) < slots

    def pack(phase, slot, half):
        def body(g, _):
            for u in range(4):
                m = g * 4 + u
                start = (2 * m + half) * TURN_PITCH
                for part in range(2):
                    rows = pl.ds(start + part * inputs, inputs)
                    value = turn[slot, rows, :] + jnp.where(first_lanes, extra[rows, :], 0.0)
                    spec[phase, m, :, part * frames : (part + 1) * frames] = value.astype(jnp.bfloat16)
            return 0

        lax.fori_loop(0, NC // 16, body, 0)

    row = pl.ds(pl.multiple_of(chan * inputs, inputs), inputs)

    def landing(phase):
        return last_ref if phase == 3 else landed.at[phase]

    def send(phase):
        shift_x, shift_core = phase & 1, phase >> 1
        if phase == 0:
            pltpu.make_async_copy(spec.at[0, chan], landing(0).at[row, :], recv_sem.at[0]).start()

        def body(r, _):
            q = r ^ 5
            base, tb = place(shift_x + 2 * (q & 1), q >> 1, shift_core)
            for dz in (4, 3, 5, 2, 6, 1, 7, 0):
                tc = base | along[dz]

                def copy():
                    pltpu.make_async_remote_copy(
                        src_ref=spec.at[phase, tc],
                        dst_ref=landing(phase).at[row, :],
                        send_sem=send_sem,
                        recv_sem=recv_sem.at[phase],
                        device_id=(tc, tb),
                        device_id_type=MESH,
                    ).start()

                if dz or phase:
                    copy()
                else:
                    pl.when(q > 0)(copy)
            return 0

        lax.fori_loop(0, 8, body, 0)

    tail_load.wait()
    tail_out[...] = tail[...].astype(jnp.bfloat16)
    pairs = inputs // 2
    transform(0, core, 0, pairs // 2)
    pl.semaphore_wait(barrier, 38)
    for dz in (4, 3, 5, 2, 6, 1, 7):
        signal(plane_sem, mine | along[dz], blk)
    onward = pltpu.make_async_remote_copy(
        src_ref=tail_out,
        dst_ref=halo,
        send_sem=halo_sem.at[0],
        recv_sem=halo_sem.at[1],
        device_id=(chan, jnp.minimum(blk + 1, blocks - 1)),
        device_id_type=MESH,
    )

    @pl.when(blk < blocks - 1)
    def _():
        onward.start()

    transform(0, core, pairs // 2, pairs)
    transform(1, core ^ 1, 0, EARLY)

    @pl.when(blk > 0)
    def _():
        onward.wait_recv()
        for f in range(HISTORY):
            value = None
            for t in range(HISTORY - f):
                earlier = halo[:, (f + t) * FFT : (f + t + 1) * FFT].astype(jnp.float32)
                value = taps[t] * earlier if value is None else value + taps[t] * earlier
            place_frame(head, f, slots, value)

    for group in range(2):
        if group:
            transform(1, core ^ 1, EARLY, pairs)
        patch(core ^ group)
        for shift_x in range(2):
            phase = group * 2 + shift_x
            pack(phase, group, (blk >> 1) ^ shift_x)
            if phase == 0:
                pl.semaphore_wait(plane_sem, 7)
            send(phase)

    @pl.when(blk < blocks - 1)
    def _():
        onward.wait_send()

    def accumulate(phase):
        source = landed.at[phase]
        step = 256

        def body(r, _):
            rows = pl.ds(pl.multiple_of(r * step, step), step)
            left = source[rows, :]
            swapped = jnp.concatenate([left[:, frames:], -left[:, :frames]], axis=1)
            for operand, out in ((left, re_ref), (swapped, im_ref)):
                value = lax.dot_general(
                    operand, source[...], (((1,), (1,)), ((), ())), preferred_element_type=jnp.float32
                )
                if phase == 0:
                    out[rows, :] = value
                else:
                    out[rows, :] += value
            return 0

        lax.fori_loop(0, NI // step, body, 0)

    for phase in range(4):
        block = landing(phase)
        pltpu.make_async_copy(block, block, recv_sem.at[phase]).wait()
        if phase < 3:
            accumulate(phase)
    pltpu.make_async_copy(landed, landed, send_sem).wait()
    sent = spec.at[0, pl.ds(0, NC // 4 - 1)]
    pltpu.make_async_copy(sent, sent, send_sem).wait()


def exchange(voltages, table):
    inputs, samples = voltages.shape
    frames = samples // FFT
    chunks = 4
    hbm = pl.BlockSpec(memory_space=pltpu.HBM)
    vmem = pl.BlockSpec(memory_space=pltpu.VMEM)
    square = jax.ShapeDtypeStruct((NI, NI), jnp.float32)
    return pl.pallas_call(
        functools.partial(exchange_kernel, frames),
        out_shape=(jax.ShapeDtypeStruct((NI, 2 * frames), jnp.bfloat16), square, square),
        in_specs=[hbm, hbm],
        out_specs=(vmem, vmem, vmem),
        scratch_shapes=[
            pltpu.VMEM((inputs, samples), jnp.int32),
            pltpu.VMEM(table.shape, jnp.float32),
            pltpu.VMEM((2, 2 * NC, HALF), jnp.bfloat16),
            pltpu.VMEM((inputs, HISTORY * FFT), jnp.int32),
            pltpu.VMEM((inputs, HISTORY * FFT), jnp.bfloat16),
            pltpu.VMEM((inputs, HISTORY * FFT), jnp.bfloat16),
            pltpu.VMEM((FFT // 128, inputs * FOLD_PITCH, 128), jnp.float32),
            pltpu.VMEM((FFT // 128, 128, 128), jnp.float32),
            pltpu.VMEM((2, NC // 2 * TURN_PITCH, frames), jnp.float32),
            pltpu.VMEM((NC // 2 * TURN_PITCH, frames), jnp.float32),
            pltpu.VMEM((4, NC // 4, inputs, 2 * frames), jnp.bfloat16),
            pltpu.VMEM((3, NI, 2 * frames), jnp.bfloat16),
            pltpu.SemaphoreType.DMA((chunks + 2,)),
            pltpu.SemaphoreType.DMA((2,)),
            pltpu.SemaphoreType.REGULAR,
            pltpu.SemaphoreType.DMA,
            pltpu.SemaphoreType.DMA((4,)),
        ],
        compiler_params=pltpu.CompilerParams(
            collective_id=0, has_side_effects=True, vmem_limit_bytes=44 * 1024 * 1024
        ),
        name="filterbank_exchange",
    )(voltages, table)


def finish_kernel(frames, total, step, last_ref, re_in, im_in, re_ref, im_ref):
    rows = pl.ds(pl.multiple_of(pl.program_id(0) * step, step), step)
    left = last_ref[rows, :]
    swapped = jnp.concatenate([left[:, frames:], -left[:, :frames]], axis=1)
    for operand, partial, out in ((left, re_in, re_ref), (swapped, im_in, im_ref)):
        value = lax.dot_general(
            operand, last_ref[...], (((1,), (1,)), ((), ())), preferred_element_type=jnp.float32
        )
        out[0] = (partial[rows, :] + value) * (1.0 / total)


def finish(last, real, imag, frames):
    step = 256
    shape = jax.ShapeDtypeStruct((1, NI, NI), jnp.float32)
    out = pl.BlockSpec((1, step, NI), lambda i: (0, i, 0))
    vmem = pl.BlockSpec(memory_space=pltpu.VMEM)
    return pl.pallas_call(
        functools.partial(finish_kernel, frames, 4 * frames, step),
        out_shape=(shape, shape),
        grid=(NI // step,),
        in_specs=[vmem, vmem, vmem],
        out_specs=(out, out),
        compiler_params=pltpu.CompilerParams(vmem_limit_bytes=24 * 1024 * 1024),
        name="finish",
    )(last, real, imag)


def local(voltages):
    frames = voltages.shape[1] // FFT
    last, real, imag = exchange(voltages, pltpu.with_memory_space_constraint(jnp.asarray(tables()), pltpu.HBM))
    return finish(last, real, imag, frames)


def solution(mesh):
    return jax.shard_map(
        local,
        mesh=mesh,
        in_specs=(P("chan", "blk"),),
        out_specs=(P(("chan", "blk"), None, None), P(("chan", "blk"), None, None)),
        check_vma=False,
    )
```

```python
import functools

import jax
import jax.numpy as jnp
import numpy as np
from jax import lax
from jax.experimental import pallas as pl
from jax.experimental.pallas import tpu as pltpu
from jax.sharding import PartitionSpec as P

NI = 1024
NC = 256
TAPS = 4
FFT = 512
HALF = FFT // 2
HISTORY = TAPS - 1
MESH = pl.DeviceIdType.MESH


def tables():
    length = TAPS * FFT
    points = np.arange(length, dtype=np.float64)
    window = 0.54 - 0.46 * np.cos(2.0 * np.pi * points / (length - 1))
    taps = (np.sinc((points - (length - 1) / 2.0) / FFT) * window).reshape(TAPS, FFT)
    scale = 1.0 / (56.0 * np.sqrt(FFT * np.mean(np.sum(taps * taps, axis=0))))
    weights = []
    for parity in range(2):
        channel = np.arange(parity, NC, 2)[:, None]
        angle = (channel * np.arange(HALF)[None, :] % FFT) * (2.0 * np.pi / FFT)
        weights.append(scale * np.concatenate([np.cos(angle), -np.sin(angle)], axis=0))
    return np.concatenate([*weights, taps.reshape(2 * TAPS, HALF)], axis=0).astype(np.float32)


FOLD_PITCH = 132
TURN_PITCH = 36
EARLY = 2


def exchange_kernel(
    frames,
    v_hbm,
    table_hbm,
    last_ref,
    re_ref,
    im_ref,
    vb,
    table,
    w_ref,
    tail,
    tail_out,
    halo,
    fold,
    head,
    turn,
    extra,
    spec,
    landed,
    in_sem,
    halo_sem,
    plane_sem,
    send_sem,
    recv_sem,
):
    inputs = v_hbm.shape[0]
    chan = lax.axis_index("chan")
    blk = lax.axis_index("blk")
    blocks = lax.axis_size("blk")
    chunks = in_sem.shape[0] - 2
    per = frames // chunks
    lead = HISTORY * FFT
    table_load = pltpu.make_async_copy(table_hbm, table, in_sem.at[chunks])
    tail_load = pltpu.make_async_copy(v_hbm.at[:, pl.ds(frames * FFT - lead, lead)], tail, in_sem.at[chunks + 1])
    loads = []
    for c in range(chunks):
        span = pl.ds(c * per * FFT, per * FFT)
        loads.append(pltpu.make_async_copy(v_hbm.at[:, span], vb.at[:, span], in_sem.at[c]))
    for load in (table_load, *loads, tail_load):
        load.start()

    z = chan & 7
    y = (chan >> 4) & 3
    x = ((chan >> 3) & 1) * 2 + (blk >> 1)
    core = blk & 1
    along = [(z + dz) & 7 for dz in range(8)]

    def place(dx, dy, dc):
        tx = (x + dx) & 3
        return (((y + dy) & 3) << 4) | ((tx >> 1) << 3), ((tx & 1) << 1) | (core ^ dc)

    barrier = pltpu.get_barrier_semaphore()

    mine = chan & ~7

    def signal(semaphore, tc, tb):
        pl.semaphore_signal(semaphore, inc=1, device_id=(tc, tb), device_id_type=MESH)

    for dz in (4, 3, 5, 2, 6, 1, 7):
        signal(barrier, mine | along[dz], blk)

    def greet(r, _):
        base, tb = place(r & 3, (r >> 2) & 3, r >> 4)
        signal(barrier, base | z, tb)
        return 0

    lax.fori_loop(1, 32, greet, 0)

    head[...] = jnp.zeros_like(head)
    table_load.wait()
    for parity in range(2):
        value = table[pl.ds(parity * 2 * (NC // 2), NC), :]
        high = value.astype(jnp.bfloat16)
        w_ref[parity, 0:NC, :] = high
        w_ref[parity, NC : 2 * NC, :] = (value - high.astype(jnp.float32)).astype(jnp.bfloat16)

    def tap(t):
        row = 2 * NC + 2 * t
        return jnp.concatenate([table[row : row + 1, :], table[row + 1 : row + 2, :]], axis=1)

    taps = [tap(t) for t in range(TAPS)]

    def place_frame(ref, f, pitch, value):
        folded = (value[:, :HALF] + value[:, HALF:], value[:, :HALF] - value[:, HALF:])
        for parity in range(2):
            for lane in range(HALF // 128):
                ref[parity * 2 + lane, pl.ds(f, inputs, stride=pitch), :] = folded[parity][
                    :, lane * 128 : (lane + 1) * 128
                ]

    def filter_frames(g, window):
        window = list(window)
        for u in range(4):
            f = g * 4 + u
            window.append(vb[:, pl.ds(pl.multiple_of(f * FFT, FFT), FFT)].astype(jnp.float32))
            value = taps[0] * window[0]
            for t in range(1, TAPS):
                value = value + taps[t] * window[t]
            window = window[1:]
            place_frame(fold, f, FOLD_PITCH, value)
        return tuple(window)

    window = tuple(jnp.zeros((inputs, FFT), jnp.float32) for _ in range(HISTORY))
    for c in range(chunks):
        loads[c].wait()
        window = lax.fori_loop(c * per // 4, (c + 1) * per // 4, filter_frames, window)

    def spectra(parity, value):
        high = value.astype(jnp.bfloat16)
        low = (value - high.astype(jnp.float32)).astype(jnp.bfloat16)
        contract = (((1,), (1,)), ((), ()))
        both = lax.dot_general(w_ref[parity], high, contract, preferred_element_type=jnp.float32)
        rest = lax.dot_general(w_ref[parity, 0:NC, :], low, contract, preferred_element_type=jnp.float32)
        return both[0:NC] + (both[NC : 2 * NC] + rest)

    def transform(slot, parity, first, last):
        def body(p, _):
            base = pl.multiple_of(p * 2 * FOLD_PITCH, 8)
            halves = []
            for lane in range(HALF // 128):
                source = fold.at[parity * 2 + lane]
                halves.append(
                    jnp.concatenate(
                        [source[pl.ds(base, frames), :], source[pl.ds(base + FOLD_PITCH, frames), :]], axis=0
                    )
                )
            out = spectra(parity, jnp.concatenate(halves, axis=1))
            for h in range(2):
                for part in range(2):
                    turn[slot, pl.ds(part * inputs + p * 2 + h, NC // 2, stride=TURN_PITCH), :] = out[
                        part * NC // 2 : (part + 1) * NC // 2, h * frames : (h + 1) * frames
                    ]
            return 0

        lax.fori_loop(first, last, body, 0)

    slots = head.shape[1] // inputs

    def patch(parity):
        out = spectra(parity, jnp.concatenate([head[parity * 2], head[parity * 2 + 1]], axis=1))
        for i in range(inputs):
            for part in range(2):
                value = out[part * NC // 2 : (part + 1) * NC // 2, :]
                if i:
                    value = pltpu.roll(value, 128 - slots * i, 1)
                extra[pl.ds(part * inputs + i, NC // 2, stride=TURN_PITCH), :] = value

    first_lanes = lax.broadcasted_iota(jnp.int32, (inputs, frames), 1) < slots

    def pack(phase, slot, half):
        def body(g, _):
            for u in range(4):
                m = g * 4 + u
                start = (2 * m + half) * TURN_PITCH
                for part in range(2):
                    rows = pl.ds(start + part * inputs, inputs)
                    value = turn[slot, rows, :] + jnp.where(first_lanes, extra[rows, :], 0.0)
                    spec[phase, m, :, part * frames : (part + 1) * frames] = value.astype(jnp.bfloat16)
            return 0

        lax.fori_loop(0, NC // 16, body, 0)

    row = pl.ds(pl.multiple_of(chan * inputs, inputs), inputs)

    def landing(phase):
        return last_ref if phase == 3 else landed.at[phase]

    def send(phase):
        shift_x, shift_core = phase & 1, phase >> 1
        if phase == 0:
            pltpu.make_async_copy(spec.at[0, chan], landing(0).at[row, :], recv_sem.at[0]).start()

        def body(r, _):
            base, tb = place(shift_x + 2 * (r & 1), r >> 1, shift_core)
            for dz in (0, 1, 2, 3, 4, 5, 6, 7):
                tc = base | along[dz]

                def copy():
                    pltpu.make_async_remote_copy(
                        src_ref=spec.at[phase, tc],
                        dst_ref=landing(phase).at[row, :],
                        send_sem=send_sem,
                        recv_sem=recv_sem.at[phase],
                        device_id=(tc, tb),
                        device_id_type=MESH,
                    ).start()

                if dz or phase:
                    copy()
                else:
                    pl.when(r > 0)(copy)
            return 0

        lax.fori_loop(0, 8, body, 0)

    tail_load.wait()
    tail_out[...] = tail[...].astype(jnp.bfloat16)
    pairs = inputs // 2
    transform(0, core, 0, pairs // 2)
    pl.semaphore_wait(barrier, 38)
    for dz in (4, 3, 5, 2, 6, 1, 7):
        signal(plane_sem, mine | along[dz], blk)
    onward = pltpu.make_async_remote_copy(
        src_ref=tail_out,
        dst_ref=halo,
        send_sem=halo_sem.at[0],
        recv_sem=halo_sem.at[1],
        device_id=(chan, jnp.minimum(blk + 1, blocks - 1)),
        device_id_type=MESH,
    )

    @pl.when(blk < blocks - 1)
    def _():
        onward.start()

    transform(0, core, pairs // 2, pairs)
    transform(1, core ^ 1, 0, EARLY)

    @pl.when(blk > 0)
    def _():
        onward.wait_recv()
        for f in range(HISTORY):
            value = None
            for t in range(HISTORY - f):
                earlier = halo[:, (f + t) * FFT : (f + t + 1) * FFT].astype(jnp.float32)
                value = taps[t] * earlier if value is None else value + taps[t] * earlier
            place_frame(head, f, slots, value)

    for group in range(2):
        if group:
            transform(1, core ^ 1, EARLY, pairs)
        patch(core ^ group)
        for shift_x in range(2):
            phase = group * 2 + shift_x
            pack(phase, group, (blk >> 1) ^ shift_x)
            if phase == 0:
                pl.semaphore_wait(plane_sem, 7)
            send(phase)

    @pl.when(blk < blocks - 1)
    def _():
        onward.wait_send()

    def accumulate(phase):
        source = landed.at[phase]
        step = 256

        def body(r, _):
            rows = pl.ds(pl.multiple_of(r * step, step), step)
            left = source[rows, :]
            swapped = jnp.concatenate([left[:, frames:], -left[:, :frames]], axis=1)
            for operand, out in ((left, re_ref), (swapped, im_ref)):
                value = lax.dot_general(
                    operand, source[...], (((1,), (1,)), ((), ())), preferred_element_type=jnp.float32
                )
                if phase == 0:
                    out[rows, :] = value
                else:
                    out[rows, :] += value
            return 0

        lax.fori_loop(0, NI // step, body, 0)

    for phase in range(4):
        block = landing(phase)
        pltpu.make_async_copy(block, block, recv_sem.at[phase]).wait()
        if phase < 3:
            accumulate(phase)
    pltpu.make_async_copy(landed, landed, send_sem).wait()
    sent = spec.at[0, pl.ds(0, NC // 4 - 1)]
    pltpu.make_async_copy(sent, sent, send_sem).wait()


def exchange(voltages, table):
    inputs, samples = voltages.shape
    frames = samples // FFT
    chunks = 4
    hbm = pl.BlockSpec(memory_space=pltpu.HBM)
    vmem = pl.BlockSpec(memory_space=pltpu.VMEM)
    square = jax.ShapeDtypeStruct((NI, NI), jnp.float32)
    return pl.pallas_call(
        functools.partial(exchange_kernel, frames),
        out_shape=(jax.ShapeDtypeStruct((NI, 2 * frames), jnp.bfloat16), square, square),
        in_specs=[hbm, hbm],
        out_specs=(vmem, vmem, vmem),
        scratch_shapes=[
            pltpu.VMEM((inputs, samples), jnp.int32),
            pltpu.VMEM(table.shape, jnp.float32),
            pltpu.VMEM((2, 2 * NC, HALF), jnp.bfloat16),
            pltpu.VMEM((inputs, HISTORY * FFT), jnp.int32),
            pltpu.VMEM((inputs, HISTORY * FFT), jnp.bfloat16),
            pltpu.VMEM((inputs, HISTORY * FFT), jnp.bfloat16),
            pltpu.VMEM((FFT // 128, inputs * FOLD_PITCH, 128), jnp.float32),
            pltpu.VMEM((FFT // 128, 128, 128), jnp.float32),
            pltpu.VMEM((2, NC // 2 * TURN_PITCH, frames), jnp.float32),
            pltpu.VMEM((NC // 2 * TURN_PITCH, frames), jnp.float32),
            pltpu.VMEM((4, NC // 4, inputs, 2 * frames), jnp.bfloat16),
            pltpu.VMEM((3, NI, 2 * frames), jnp.bfloat16),
            pltpu.SemaphoreType.DMA((chunks + 2,)),
            pltpu.SemaphoreType.DMA((2,)),
            pltpu.SemaphoreType.REGULAR,
            pltpu.SemaphoreType.DMA,
            pltpu.SemaphoreType.DMA((4,)),
        ],
        compiler_params=pltpu.CompilerParams(
            collective_id=0, has_side_effects=True, vmem_limit_bytes=44 * 1024 * 1024
        ),
        name="filterbank_exchange",
    )(voltages, table)


def finish_kernel(frames, total, step, last_ref, re_in, im_in, re_ref, im_ref):
    rows = pl.ds(pl.multiple_of(pl.program_id(0) * step, step), step)
    left = last_ref[rows, :]
    swapped = jnp.concatenate([left[:, frames:], -left[:, :frames]], axis=1)
    for operand, partial, out in ((left, re_in, re_ref), (swapped, im_in, im_ref)):
        value = lax.dot_general(
            operand, last_ref[...], (((1,), (1,)), ((), ())), preferred_element_type=jnp.float32
        )
        out[0] = (partial[rows, :] + value) * (1.0 / total)


def finish(last, real, imag, frames):
    step = 256
    shape = jax.ShapeDtypeStruct((1, NI, NI), jnp.float32)
    out = pl.BlockSpec((1, step, NI), lambda i: (0, i, 0))
    vmem = pl.BlockSpec(memory_space=pltpu.VMEM)
    return pl.pallas_call(
        functools.partial(finish_kernel, frames, 4 * frames, step),
        out_shape=(shape, shape),
        grid=(NI // step,),
        in_specs=[vmem, vmem, vmem],
        out_specs=(out, out),
        compiler_params=pltpu.CompilerParams(vmem_limit_bytes=24 * 1024 * 1024),
        name="finish",
    )(last, real, imag)


def local(voltages):
    frames = voltages.shape[1] // FFT
    last, real, imag = exchange(voltages, pltpu.with_memory_space_constraint(jnp.asarray(tables()), pltpu.HBM))
    return finish(last, real, imag, frames)


def solution(mesh):
    return jax.shard_map(
        local,
        mesh=mesh,
        in_specs=(P("chan", "blk"),),
        out_specs=(P(("chan", "blk"), None, None), P(("chan", "blk"), None, None)),
        check_vma=False,
    )
```
